32 devices in a mesh: rep: 4 (over y, core), fsdp: 8 (over z, x).
Axes of the slice: x: 2, y: 2, z: 4, core: 2. Of those that a mesh axis runs over, the one named last changes fastest.
Arguments:
- query_rows: bfloat16 [4, 3072, 2560], P('rep', 'fsdp'), may hold values from -5 to 5
- key_rows: bfloat16 [4, 3072, 2560], P('rep', 'fsdp'), may hold values from -5 to 5
- value_rows: bfloat16 [4, 3072, 2560], P('rep', 'fsdp'), may hold values from -5 to 5
- residual_in: bfloat16 [4, 3072, 2560], P('rep', 'fsdp'), may hold values from -6 to 6
- out_grad: bfloat16 [4, 3072, 2560], P('rep', 'fsdp'), may hold values from -6 to 6
- doc_ids: int32 [4, 3072], P('rep', 'fsdp'), may hold values from 0 to 47, never falling along the last dimension, each value on 1 to 256 neighbouring positions
- out_weight: bfloat16 [4, 2560, 2560], P('rep', 'fsdp'), may hold values from -0.125 to 0.125
- momentum: float32 [4, 2560, 2560], P('rep', 'fsdp'), may hold values from -192 to 192
- step_index: int32 [1], replicated, may hold values from 0 to 63
Outputs:
- block_out: bfloat16 [4, 3072, 2560], P('rep', 'fsdp')
- query_grad: bfloat16 [4, 3072, 2560], P('rep', 'fsdp')
- key_grad: bfloat16 [4, 3072, 2560], P('rep', 'fsdp')
- value_grad: bfloat16 [4, 3072, 2560], P('rep', 'fsdp')
- new_weight: bfloat16 [4, 2560, 2560], P('rep', 'fsdp')
- new_momentum: float32 [4, 2560, 2560], P('rep', 'fsdp')
The draws below stay inside these ranges and needn't reach their ends.
All inputs are finite; a program needn't handle non-finite values.
Results may differ from the reference program's by a relative error of at most 0.018.
Values may be sent and summed in bfloat16 or wider, within the bound.
A program may use at most 192 MiB of HBM per device.

```python
import math
import jax
import jax.numpy as jnp
import numpy as np
from jax import lax

D = 2560
HEADS = 20
HEAD_SIZE = 128
TOK_DEV = 384
HD = 2560
TOKENS = 3072
N_REP = 4


def query_key_pair(key):
    shape = (N_REP, TOKENS, HD)
    first = jax.random.fold_in(key, 11)
    second = jax.random.fold_in(key, 12)
    queries = jnp.clip(jax.random.normal(first, shape, jnp.float32), -5.0, 5.0)
    keyset = jnp.clip(jax.random.normal(second, shape, jnp.float32), -5.0, 5.0)
    return (queries, keyset)


def draw_query_rows(key, part):
    return query_key_pair(key)[0].astype(jnp.bfloat16)


def draw_key_rows(key, part):
    return query_key_pair(key)[1].astype(jnp.bfloat16)


def block_scale(own_key, extent, split, least, top_value):
    def one(position, blocks):
        heights = jax.random.uniform(jax.random.fold_in(jax.random.fold_in(own_key, 6), position), (blocks,), jnp.float32, least / len(split), top_value / len(split))
        return jnp.repeat(jnp.exp(heights), extent[position] // blocks).reshape((-1,) + (1,) * (len(extent) - position - 1))

    gain = one(*split[0])
    for cut in split[1:]:
        gain = gain * one(*cut)
    return gain


def length_profile(count, total, reach, lean):
    portions = [(1 << 20) // math.isqrt(rank ** lean) + 1 for rank in range(2, count + 1)]
    surplus, counts = total - reach - (count - 1), [1] * (count - 1)
    while surplus > 0:
        free = [i for i in range(count - 1) if counts[i] < reach]
        pool, left = sum([portions[i] for i in free]), surplus
        for i in free:
            addition = min(reach - counts[i], max(1, left * portions[i] // pool), surplus)
            counts[i] = counts[i] + addition
            surplus = surplus - addition
    return np.array([reach] + counts)


def uneven_parts(own_key, count, total, most, lean):
    if count == 2:
        one = jax.random.randint(own_key, (), max(1, total - most), min(most, total - 1) + 1)
        return jnp.stack([one, total - one])
    sizes = jnp.asarray(length_profile(count, total, most, lean), jnp.int32)
    couples = (count - 1) // 2
    source_of, taker = sizes[1:1 + 2 * couples:2], sizes[2:2 + 2 * couples:2]
    slack = jnp.minimum(source_of - 1, most - taker)
    moved = jax.random.randint(jax.random.fold_in(own_key, 1), (couples,), 0, 1 << 20) % (slack + 1)
    sizes = sizes.at[1:1 + 2 * couples:2].set(source_of - moved).at[2:2 + 2 * couples:2].set(taker + moved)
    return sizes[jax.random.permutation(jax.random.fold_in(own_key, 2), count)]


def bell_draw(own_key, dims, deviation, most, cuts=(), kind=jnp.bfloat16):
    values = deviation * jax.random.normal(own_key, dims, jnp.float32)
    if cuts:
        values = values * block_scale(own_key, dims, cuts, -0.22, 0.18)
    return jnp.clip(values, -most, most).astype(kind)


def setup_inputs(seed: int = 0) -> dict:
    streams_of = jax.random.split(jax.random.key(seed), 10)
    query_rows = draw_query_rows(jax.random.fold_in(streams_of[9], 71), 0)
    key_rows = draw_key_rows(jax.random.fold_in(streams_of[9], 71), 0)
    value_rows = bell_draw(streams_of[2], (N_REP, TOKENS, HD), 1.0, 5.0, ((0, 4), (1, 8)))
    residual_in = bell_draw(streams_of[3], (N_REP, TOKENS, D), 1.0, 6.0, ((0, 4), (1, 8)))
    out_grad = bell_draw(streams_of[4], (N_REP, TOKENS, D), 1.0, 6.0, ((0, 4), (1, 8)))
    doc_ids = jax.vmap(lambda own: jnp.searchsorted(jnp.cumsum(uneven_parts(own, max(4, TOKENS // 64), TOKENS, min(256, TOKENS // 2), 1)), jnp.arange(TOKENS), side="right"))(jax.random.split(streams_of[5], N_REP)).reshape((N_REP, TOKENS)).astype(jnp.int32)
    out_weight = bell_draw(streams_of[6], (N_REP, HD, D), HD ** -0.5, 0.125, ((0, 4), (1, 8)))
    momentum = bell_draw(streams_of[7], (N_REP, HD, D), 32.0, 192.0, ((0, 4), (1, 8)), jnp.float32)
    step_index = jax.random.randint(streams_of[8], (1,), 0, 64).astype(jnp.int32)
    return {"query_rows": query_rows, "key_rows": key_rows, "value_rows": value_rows, "residual_in": residual_in, "out_grad": out_grad, "doc_ids": doc_ids, "out_weight": out_weight, "momentum": momentum, "step_index": step_index}


momentum_decay = 0.9
learning_rate = 0.0003


def rounded(values):
    return lax.optimization_barrier(values.astype(jnp.bfloat16)).astype(jnp.float32)


def attend(query_block, key_block, value_block, doc_block):
    length = query_block.shape[0]
    score_scale = HEAD_SIZE ** -0.5
    query_heads = query_block.astype(jnp.float32).reshape(length, HEADS, HEAD_SIZE)
    key_heads = key_block.astype(jnp.float32).reshape(length, HEADS, HEAD_SIZE)
    value_heads = value_block.astype(jnp.float32).reshape(length, HEADS, HEAD_SIZE)
    scores = jnp.einsum("qhd,khd->hqk", query_heads, key_heads) * score_scale
    places = jnp.arange(length, dtype=jnp.int32)
    allowed = (places[None, :] <= places[:, None]) & (doc_block[:, None] == doc_block[None, :])
    scores = jnp.where(allowed[None], scores, -jnp.inf)
    row_peaks = jnp.max(scores, axis=-1, keepdims=True)
    exponents = jnp.exp(scores - row_peaks)
    attn_probs = exponents / jnp.sum(exponents, axis=-1, keepdims=True)
    probs_low = rounded(attn_probs)
    context = jnp.einsum("hqk,khd->qhd", probs_low, value_heads)
    context = context.reshape(length, HEADS * HEAD_SIZE).astype(jnp.bfloat16)
    return context, attn_probs, probs_low, query_heads, key_heads, value_heads


def attend_back(context_grad, attn_probs, probs_low, query_heads, key_heads, value_heads):
    length = query_heads.shape[0]
    score_scale = HEAD_SIZE ** -0.5
    grad_heads = context_grad.astype(jnp.float32).reshape(length, HEADS, HEAD_SIZE)
    value_grad = jnp.einsum("hqk,qhd->khd", probs_low, grad_heads)
    prob_grad = jnp.einsum("qhd,khd->hqk", grad_heads, value_heads)
    row_delta = jnp.sum(prob_grad * attn_probs, axis=-1, keepdims=True)
    score_grad = rounded(attn_probs * (prob_grad - row_delta) * score_scale)
    query_grad = jnp.einsum("hqk,khd->qhd", score_grad, key_heads)
    key_grad = jnp.einsum("hqk,qhd->khd", score_grad, query_heads)
    width = HEADS * HEAD_SIZE
    return (query_grad.reshape(length, width).astype(jnp.bfloat16),
            key_grad.reshape(length, width).astype(jnp.bfloat16),
            value_grad.reshape(length, width).astype(jnp.bfloat16))


def reference(query_rows, key_rows, value_rows, residual_in, out_grad, doc_ids, out_weight, momentum, step_index):
    hidden = HEADS * HEAD_SIZE
    blocks = TOKENS // TOK_DEV
    outputs_block, outputs_query, outputs_key, outputs_value = [], [], [], []
    moments, stepped_all = [], []
    for replica in range(N_REP):
        weight = out_weight[replica]

        def one_block(running, pieces):
            query_block, key_block, value_block, resid_block, grad_block, doc_block = pieces
            context, attn_probs, probs_low, query_heads, key_heads, value_heads = attend(query_block, key_block, value_block, doc_block)
            projected = jnp.dot(context, weight, preferred_element_type=jnp.float32)
            block_out = (resid_block.astype(jnp.float32) + projected).astype(jnp.bfloat16)
            context_grad = lax.dot_general(grad_block, weight, (((1,), (1,)), ((), ())), preferred_element_type=jnp.float32).astype(jnp.bfloat16)
            query_grad, key_grad, value_grad = attend_back(context_grad, attn_probs, probs_low, query_heads, key_heads, value_heads)
            weight_term = lax.dot_general(context, grad_block, (((0,), (0,)), ((), ())), preferred_element_type=jnp.float32)
            return running + rounded(weight_term), (block_out, query_grad, key_grad, value_grad)

        def per_block(array):
            return array[replica].reshape((blocks, TOK_DEV) + array.shape[2:])

        pieces = (per_block(query_rows), per_block(key_rows), per_block(value_rows),
                  per_block(residual_in), per_block(out_grad), per_block(doc_ids))
        weight_grad, results = lax.scan(one_block, jnp.zeros((hidden, D), jnp.float32), pieces)
        outputs_block.append(results[0].reshape(TOKENS, D))
        outputs_query.append(results[1].reshape(TOKENS, hidden))
        outputs_key.append(results[2].reshape(TOKENS, hidden))
        outputs_value.append(results[3].reshape(TOKENS, hidden))
        new_momentum = momentum_decay * momentum[replica] + weight_grad
        moments.append(new_momentum)
        stepped_all.append((weight.astype(jnp.float32) - learning_rate * new_momentum).astype(jnp.bfloat16))
    stepped = jnp.stack(stepped_all)
    levels = N_REP.bit_length() - 1
    chosen_level = (step_index[0] % levels).astype(jnp.int32)
    partner = jnp.bitwise_xor(jnp.arange(N_REP, dtype=jnp.int32), jnp.left_shift(jnp.ones((), jnp.int32), chosen_level))
    new_weight = ((stepped.astype(jnp.float32) + stepped[partner].astype(jnp.float32)) * 0.5).astype(jnp.bfloat16)
    return (jnp.stack(outputs_block), jnp.stack(outputs_query), jnp.stack(outputs_key),
            jnp.stack(outputs_value), new_weight, jnp.stack(moments))
```

```python
import functools

import jax
import jax.numpy as jnp
from jax import lax
from jax.experimental import pallas as pl
from jax.experimental.pallas import tpu as pltpu
from jax.sharding import PartitionSpec as P

HEAD_SIZE = 128

momentum_decay = 0.9
learning_rate = 0.0003


def swapped(block, axis, distance):
    count = lax.axis_size(axis)
    route = []
    for low in range(count):
        high = low | 1 << distance
        if high != low and high < count:
            route += [(low, high), (high, low)]
    return lax.ppermute(block, axis, route)


def probabilities(q, k, doc_column, doc_row):
    length = q.shape[0]
    scores = lax.dot_general(
        q, k, (((1,), (1,)), ((), ())), preferred_element_type=jnp.float32
    ) * (HEAD_SIZE ** (-0.5))
    rows = lax.broadcasted_iota(jnp.int32, (length, length), 0)
    columns = lax.broadcasted_iota(jnp.int32, (length, length), 1)
    allowed = (columns <= rows) & (doc_column == doc_row)
    scores = jnp.where(allowed, scores, -jnp.inf)
    exponents = jnp.exp(scores - jnp.max(scores, axis=-1, keepdims=True))
    return exponents / jnp.sum(exponents, axis=-1, keepdims=True)


def forward_kernel(q_ref, k_ref, v_ref, doc_column_ref, doc_row_ref, context_ref):
    for head in range(q_ref.shape[1] // HEAD_SIZE):
        cut = slice(head * HEAD_SIZE, (head + 1) * HEAD_SIZE)
        probs = probabilities(q_ref[:, cut], k_ref[:, cut], doc_column_ref[...], doc_row_ref[...])
        context_ref[:, cut] = jnp.dot(
            probs.astype(jnp.bfloat16), v_ref[:, cut], preferred_element_type=jnp.float32
        ).astype(jnp.bfloat16)


def backward_kernel(
    q_ref, k_ref, v_ref, grad_ref, doc_column_ref, doc_row_ref, dq_ref, dk_ref, dv_ref
):
    for head in range(q_ref.shape[1] // HEAD_SIZE):
        cut = slice(head * HEAD_SIZE, (head + 1) * HEAD_SIZE)
        q, k, v, grad = q_ref[:, cut], k_ref[:, cut], v_ref[:, cut], grad_ref[:, cut]
        probs = probabilities(q, k, doc_column_ref[...], doc_row_ref[...])
        dv_ref[:, cut] = lax.dot_general(
            probs.astype(jnp.bfloat16),
            grad,
            (((0,), (0,)), ((), ())),
            preferred_element_type=jnp.float32,
        ).astype(jnp.bfloat16)
        prob_grad = lax.dot_general(
            grad, v, (((1,), (1,)), ((), ())), preferred_element_type=jnp.float32
        )
        row_delta = jnp.sum(prob_grad * probs, axis=-1, keepdims=True)
        score_grad = (probs * (prob_grad - row_delta) * (HEAD_SIZE ** (-0.5))).astype(jnp.bfloat16)
        dq_ref[:, cut] = jnp.dot(score_grad, k, preferred_element_type=jnp.float32).astype(
            jnp.bfloat16
        )
        dk_ref[:, cut] = lax.dot_general(
            score_grad, q, (((0,), (0,)), ((), ())), preferred_element_type=jnp.float32
        ).astype(jnp.bfloat16)


def per_head(kernel, arrays, doc_block, outputs, matmuls):
    length, width = arrays[0].shape
    step = 2 * HEAD_SIZE if width % (2 * HEAD_SIZE) == 0 else HEAD_SIZE
    block = pl.BlockSpec((length, step), lambda h: (0, h))
    whole = lambda shape: pl.BlockSpec(shape, lambda h: (0, 0))
    result = jax.ShapeDtypeStruct((length, width), jnp.bfloat16)
    return pl.pallas_call(
        kernel,
        grid=(width // step,),
        in_specs=[block] * len(arrays) + [whole((length, 1)), whole((1, length))],
        out_specs=[block] * outputs,
        out_shape=[result] * outputs,
        cost_estimate=pl.CostEstimate(
            flops=4 * matmuls * length * length * width,
            bytes_accessed=(len(arrays) + outputs) * length * width * 2,
            transcendentals=length * length * width // HEAD_SIZE,
        ),
    )(*arrays, doc_block[:, None], doc_block[None, :])


def on_device(
    query_rows,
    key_rows,
    value_rows,
    residual_in,
    out_grad,
    doc_ids,
    out_weight,
    momentum,
    step_index,
):
    count = lax.axis_size("fsdp")
    side = lax.axis_index("fsdp") % 2
    groups = [[i for i in range(count) if i % 2 == s] for s in range(2)]
    pair = [(i, i ^ 1) for i in range(count)]
    first = side == 0
    query, key, value = query_rows[0], key_rows[0], value_rows[0]
    weight_shard = out_weight[0]
    own_grad = out_grad[0]
    rows = weight_shard.shape[0]
    gathered = lax.all_gather(
        weight_shard, "fsdp", axis=0, tiled=True, axis_index_groups=groups
    )
    pair_grad = lax.ppermute(own_grad, "fsdp", pair)
    (context,) = per_head(forward_kernel, (query, key, value), doc_ids[0], 1, 2)

    def half(array, which):
        return jnp.concatenate(
            [array[:, j * rows : (j + 1) * rows] for j in range(which, count, 2)], axis=1
        )

    low, high = half(context, 0), half(context, 1)
    own_context = jnp.where(first, low, high)
    pair_context = lax.ppermute(jnp.where(first, high, low), "fsdp", pair)

    def outer(left, right):
        return lax.dot_general(
            left, right, (((0,), (0,)), ((), ())), preferred_element_type=jnp.float32
        )

    weight_term = (outer(own_context, own_grad) + outer(pair_context, pair_grad)).astype(
        jnp.bfloat16
    )
    weight_grad = lax.psum_scatter(
        weight_term, "fsdp", scatter_dimension=0, tiled=True, axis_index_groups=groups
    ).astype(jnp.float32)

    def back(grad):
        return lax.dot_general(
            grad, gathered, (((1,), (1,)), ((), ())), preferred_element_type=jnp.float32
        ).astype(jnp.bfloat16)

    got_back = lax.ppermute(back(pair_grad), "fsdp", pair)
    pair_out = jnp.dot(pair_context, gathered, preferred_element_type=jnp.float32)
    got_out = lax.ppermute(pair_out.astype(jnp.bfloat16), "fsdp", pair)
    own_back = back(own_grad)
    even = jnp.where(first, own_back, got_back)
    odd = jnp.where(first, got_back, own_back)
    pieces = []
    for j in range(count // 2):
        cut = slice(j * rows, (j + 1) * rows)
        pieces += [even[:, cut], odd[:, cut]]
    context_grad = jnp.concatenate(pieces, axis=1)
    query_grad, key_grad, value_grad = per_head(
        backward_kernel, (query, key, value, context_grad), doc_ids[0], 3, 5
    )
    own_out = jnp.dot(own_context, gathered, preferred_element_type=jnp.float32)
    block_out = (
        residual_in[0].astype(jnp.float32) + own_out + got_out.astype(jnp.float32)
    ).astype(jnp.bfloat16)

    new_momentum = momentum_decay * momentum[0] + weight_grad
    stepped = (weight_shard.astype(jnp.float32) - learning_rate * new_momentum).astype(jnp.bfloat16)
    levels = lax.axis_size("rep").bit_length() - 1
    branches = [functools.partial(swapped, axis="rep", distance=level) for level in range(levels)]
    partner = lax.switch(step_index[0] % levels, branches, stepped)
    new_weight = ((stepped.astype(jnp.float32) + partner.astype(jnp.float32)) * 0.5).astype(
        jnp.bfloat16
    )
    return (
        block_out[None],
        query_grad[None],
        key_grad[None],
        value_grad[None],
        new_weight[None],
        new_momentum[None],
    )


def solution(mesh):
    rows = P("rep", "fsdp", None)
    return jax.shard_map(
        on_device,
        mesh=mesh,
        in_specs=(rows, rows, rows, rows, rows, P("rep", "fsdp"), rows, rows, P()),
        out_specs=(rows,) * 6,
        check_vma=False,
    )
```
